32 devices in a mesh: grp: 2 (over x), tile: 16 (over z, y, core).
Axes of the slice: x: 2, y: 2, z: 4, core: 2. Of those that a mesh axis runs over, the one named last changes fastest.
Arguments:
- visibility: bfloat16 [32, 16, 2, 256, 256], P('tile', 'grp'), parts along dimension 1, may hold values from -12 to 12
- station_beam: bfloat16 [16, 2, 512, 2048], P('grp', None, 'tile'), parts along dimension 0, may hold values from -4.1875 to 4.1875
- antenna_uvw: float32 [16, 3, 2048], P('grp'), parts along dimension 0, may hold values from -40 to 40
- source_dirs: float32 [2, 4096], P(None, 'tile'), may hold values from -0.4 to 0.4
- source_flux: bfloat16 [8192], P(('grp', 'tile')), parts along dimension 0, may hold values from 0.0029907227 to 0.029907227
- visible_list: int32 [8, 512], P(None, 'tile'), may hold values from 0 to 255
- antenna_flags: int32 [16, 2048], P('grp'), parts along dimension 0, may hold values 0 or 1
Outputs:
- residual: bfloat16 [32, 16, 2, 256, 256], P('tile', 'grp'), parts along dimension 1
- flux_grad: float32 [16, 512], P('grp', 'tile'), parts along dimension 0
The draws below stay inside these ranges and needn't reach their ends.
There are 2 independent parts, one for each index of `grp`. The reference program is written for one: setup_inputs(seed, part) draws one part's arguments, and reference() takes and returns one part's arrays. A program takes and returns all parts, laid end to end along the dimension named above; an argument that names none is the same for every part. Nothing has to cross between parts.
Inputs may be any that keep to these rules, and one draw needn't show every extreme that they name: `visible_list`: entry k of a slot names pool source 256 * (k // 32) + value, a source of its own group. `antenna_flags`: 1 marks a flagged antenna.
All inputs are finite; a program needn't handle non-finite values.
Results may differ from the reference program's by a relative error of at most 0.0034.
Values may be sent and summed in bfloat16 or wider, within the bound.
A program may use at most 192 MiB of HBM per device.

```python
import math
import jax
import jax.numpy as jnp
import numpy as np
from jax import lax

ANTENNAS = 2048
VISIBLE = 512
SLOTS = 8
POOL_DEV = 256
BLOCKS = 8
SPAN = 256
UNITS = 32
PER_GROUP = 32
POOL = 4096


def place_ends(values, stream_key, smallest, top_value):
    longest = values.shape.index(max(values.shape))
    spots = []
    for shift in (0, 1):
        where = [jax.random.randint(jax.random.fold_in(stream_key, axis), (), 0, length) for axis, length in enumerate(values.shape)]
        where[longest] = (where[longest] + shift) % values.shape[longest]
        spots.append(tuple(where))
    return values.at[spots[0]].set(smallest).at[spots[1]].set(top_value)


def level_of(rng, shape, cuts, low, high):
    level = 1.0
    for dim, shards_of in cuts:
        draws = jax.random.uniform(jax.random.fold_in(jax.random.fold_in(rng, 6), dim), (shards_of,), jnp.float32, low / len(cuts), high / len(cuts))
        level = level * jnp.repeat(jnp.exp(draws), shape[dim] // shards_of).reshape((-1,) + (1,) * (len(shape) - 1 - dim))
    return level


def centred(stream_key, shape, scale, most, shards=(), held_as=jnp.bfloat16):
    drawn = scale * jax.random.normal(stream_key, shape, jnp.float32)
    if shards:
        drawn = drawn * level_of(stream_key, shape, shards, -0.22, 0.18)
    return jnp.clip(drawn, -most, most).astype(held_as)


def setup_inputs(seed: int = 0, part: int = 0) -> dict:
    arg_keys = jax.random.split(jax.random.key(seed), 8)
    part_keys = jax.random.split(jax.random.fold_in(arg_keys[7], part), 8)
    visibility = centred(part_keys[0], (UNITS, SLOTS, 2, SPAN, SPAN), 2.0, 12.0, ((0, 16),))
    station_beam = centred(part_keys[1], (SLOTS, 2, VISIBLE, ANTENNAS), 0.7, 4.1875, ((2, 16),))
    antenna_uvw = jnp.clip(jax.random.uniform(part_keys[2], (SLOTS, 3, ANTENNAS), jnp.float32, -40.0, 40.0), -40.0, 40.0)
    source_dirs = jnp.clip(jax.random.uniform(arg_keys[3], (2, POOL), jnp.float32, -0.4, 0.4) * level_of(arg_keys[3], (2, POOL), ((1, 16),), -0.4, 0.0), -0.4, 0.4)
    source_flux = jnp.clip(jnp.exp(math.log(0.029907227) - 2.3025851 * jax.random.uniform(part_keys[4], (POOL,), jnp.float32) ** level_of(part_keys[4], (POOL,), ((0, 16),), -0.2, 0.2)), 0.0029907227, 0.029907227).astype(jnp.bfloat16)
    visible_list = place_ends(jax.random.randint(arg_keys[5], (SLOTS, VISIBLE), 0, POOL_DEV), jax.random.fold_in(arg_keys[5], 1), 0, POOL_DEV - 1).astype(jnp.int32)
    antenna_flags = place_ends((jax.random.randint(part_keys[6], (SLOTS, ANTENNAS), 0, 10) < 1).astype(jnp.int32), jax.random.fold_in(part_keys[6], 1), 0, 1)
    return {"visibility": visibility, "station_beam": station_beam, "antenna_uvw": antenna_uvw, "source_dirs": source_dirs, "source_flux": source_flux, "visible_list": visible_list, "antenna_flags": antenna_flags}


two_pi = 2.0 * math.pi

def unit_table(block_count):
    first_list = []
    second_list = []
    diag_list = []
    for row_block in range(block_count):
        for col_block in range(row_block + 1, block_count):
            first_list.append(row_block)
            second_list.append(col_block)
            diag_list.append(0)
    for pair_index in range(block_count // 2):
        first_list.append(2 * pair_index)
        second_list.append(2 * pair_index + 1)
        diag_list.append(1)
    return (np.array(first_list, np.int32), np.array(second_list, np.int32), np.array(diag_list, np.int32))

def make_factors(station_beam, antenna_uvw, coord_east, coord_north):
    depth_term = jnp.sqrt(1.0 - coord_east * coord_east - coord_north * coord_north) - 1.0
    delay_sum = antenna_uvw[:, 0, None, :] * coord_east[:, :, None] + antenna_uvw[:, 1, None, :] * coord_north[:, :, None] + antenna_uvw[:, 2, None, :] * depth_term[:, :, None]
    phases = two_pi * delay_sum
    cosine = jnp.cos(phases)
    sine = jnp.sin(phases)
    beam_f = station_beam.astype(jnp.float32)
    real_part = beam_f[:, 0] * cosine + beam_f[:, 1] * sine
    imag_part = beam_f[:, 1] * cosine - beam_f[:, 0] * sine
    return jnp.stack([real_part, imag_part], 1).astype(jnp.bfloat16)

def predict(rows_f, cols_f, brightness):
    scaled = (rows_f.astype(jnp.float32) * brightness.astype(jnp.float32)[:, None, :, None]).astype(jnp.bfloat16)
    turned = jnp.stack([scaled[:, 1], -scaled[:, 0]], 1)
    stacked = jnp.stack([scaled, turned], 1).astype(jnp.float32)
    return jnp.einsum('tdckr,tckq->tdrq', stacked, cols_f.astype(jnp.float32))

def pull_back(resid, rows_f, cols_f):
    rstack = jnp.stack([jnp.stack([resid[:, 0], -resid[:, 1]], 1), jnp.stack([resid[:, 1], resid[:, 0]], 1)], 1).astype(jnp.float32)
    pulled = jnp.einsum('tdcrq,tckq->tdkr', rstack, cols_f.astype(jnp.float32))
    return lax.optimization_barrier(jnp.sum(rows_f.astype(jnp.float32) * pulled, axis=(1, 3)))

def reference(visibility, station_beam, antenna_uvw, source_dirs, source_flux, visible_list, antenna_flags):
    group_base = jnp.arange(VISIBLE, dtype=jnp.int32) // PER_GROUP * POOL_DEV
    pool_index = (group_base[None, :] + visible_list).astype(jnp.int32)
    coord_east = jnp.take(source_dirs[0], pool_index)
    coord_north = jnp.take(source_dirs[1], pool_index)
    brightness = jnp.take(source_flux, pool_index)
    factors = make_factors(station_beam, antenna_uvw, coord_east, coord_north)
    keep_all = 1.0 - antenna_flags.astype(jnp.float32)
    first_tab, second_tab, diag_tab = unit_table(BLOCKS)
    first_arr = jnp.asarray(first_tab)
    second_arr = jnp.asarray(second_tab)
    diag_arr = jnp.asarray(diag_tab)
    local_ids = jnp.arange(SPAN, dtype=jnp.int32)
    upper_part = local_ids[:, None] < local_ids[None, :]
    lower_part = local_ids[:, None] > local_ids[None, :]

    def one_unit(unit_id):
        start_one = (first_arr[unit_id] * SPAN).astype(jnp.int32)
        start_two = (second_arr[unit_id] * SPAN).astype(jnp.int32)
        diag_tile = diag_arr[unit_id] == 1
        block_one = lax.dynamic_slice_in_dim(factors, start_one, SPAN, 3)
        block_two = lax.dynamic_slice_in_dim(factors, start_two, SPAN, 3)
        cols_one = jnp.where(diag_tile, block_one, block_two)
        first_pred = predict(block_one, cols_one, brightness)
        second_pred = predict(block_two, block_two, brightness)
        first_mask = jnp.logical_or(jnp.logical_not(diag_tile), upper_part)
        predicted = jnp.where(first_mask[None, None], first_pred, jnp.swapaxes(second_pred, 2, 3))
        keep_one = lax.dynamic_slice_in_dim(keep_all, start_one, SPAN, 1)
        keep_two = lax.dynamic_slice_in_dim(keep_all, start_two, SPAN, 1)
        upper_f = upper_part.astype(jnp.float32)
        lower_f = lower_part.astype(jnp.float32)
        off_weight = keep_one[:, :, None] * keep_two[:, None, :]
        diag_weight = upper_f[None] * keep_one[:, :, None] * keep_one[:, None, :] + lower_f[None] * keep_two[:, :, None] * keep_two[:, None, :]
        weights = jnp.where(diag_tile, diag_weight, off_weight)
        vis_unit = lax.dynamic_index_in_dim(visibility, unit_id, 0, keepdims=False)
        residual = (weights[:, None] * (vis_unit.astype(jnp.float32) - predicted)).astype(jnp.bfloat16)
        zero_res = jnp.zeros_like(residual)
        first_res = jnp.where(first_mask[None, None], residual, zero_res)
        second_sel = jnp.logical_and(diag_tile, lower_part)
        second_res = jnp.swapaxes(jnp.where(second_sel[None, None], residual, zero_res), 2, 3)
        partial_value = pull_back(first_res, block_one, cols_one) + pull_back(second_res, block_two, block_two)
        return (residual, partial_value)
    residual, partial_value = lax.map(one_unit, jnp.arange(UNITS, dtype=jnp.int32))
    flux_grad = lax.optimization_barrier(jnp.sum(partial_value, 0)) * (-1.0 / (8.0 * ANTENNAS))
    return (residual, flux_grad)
```

```python
import functools
import math

import jax
import jax.numpy as jnp
from jax import lax
from jax.experimental import pallas as pl
from jax.experimental.pallas import tpu as pltpu
from jax.sharding import PartitionSpec as P

BLOCKS = 8
MESH = pl.DeviceIdType.MESH

two_pi = 2.0 * math.pi


def build_factors(station_beam, antenna_uvw, source_dirs, source_flux, visible_list):
    pool_size = source_dirs.shape[1]
    slots, _, per_group, antennas = station_beam.shape
    span = antennas // BLOCKS
    chosen = visible_list[:, :, None] == jnp.arange(pool_size, dtype=jnp.int32)[None, None, :]
    coord_east = jnp.sum(jnp.where(chosen, source_dirs[0][None, None, :], 0.0), axis=2)
    coord_north = jnp.sum(jnp.where(chosen, source_dirs[1][None, None, :], 0.0), axis=2)
    brightness = jnp.sum(
        jnp.where(chosen, source_flux.astype(jnp.float32)[None, None, :], 0.0), axis=2
    ).astype(jnp.bfloat16)
    depth_term = jnp.sqrt(1.0 - coord_east * coord_east - coord_north * coord_north) - 1.0
    delay_sum = (
        antenna_uvw[:, 0, None, :] * coord_east[:, :, None]
        + antenna_uvw[:, 1, None, :] * coord_north[:, :, None]
        + antenna_uvw[:, 2, None, :] * depth_term[:, :, None]
    )
    phases = two_pi * delay_sum
    cosine = jnp.cos(phases)
    sine = jnp.sin(phases)
    beam_f = station_beam.astype(jnp.float32)
    real_part = beam_f[:, 0] * cosine + beam_f[:, 1] * sine
    imag_part = beam_f[:, 1] * cosine - beam_f[:, 0] * sine
    both = jnp.stack([real_part, imag_part], 1).astype(jnp.bfloat16)
    both = both.reshape(slots, 2, per_group, BLOCKS, span).transpose(0, 3, 1, 2, 4)
    return both.reshape(slots, BLOCKS, 2 * per_group, span), brightness


def unit_blocks(unit_id):
    pairs = BLOCKS * (BLOCKS - 1) // 2
    first = jnp.int32(0)
    start = jnp.int32(0)
    offset = 0
    for row in range(1, BLOCKS - 1):
        offset += BLOCKS - row
        first = jnp.where(unit_id >= offset, jnp.int32(row), first)
        start = jnp.where(unit_id >= offset, jnp.int32(offset), start)
    second = unit_id - start + first + 1
    diag = unit_id >= pairs
    first = jnp.where(diag, 2 * (unit_id - pairs), first)
    second = jnp.where(diag, 2 * (unit_id - pairs) + 1, second)
    return first, second, diag


def kernel(
    dims, own, bright, keep, vis, res, flux,
    gath, ball, work, flx, frecv,
    r_sem, su, sd, sy, sc, lc, vsem, osem, bs, br, fs, fr,
):
    Z, Y, slots, units, per_group, span, scale = dims
    T = Z * Y * 2
    me = lax.axis_index("tile")
    core = me % 2
    y = (me // 2) % Y
    z = me // (2 * Y)

    def dev(zi, yi, ci):
        return (zi * Y + yi) * 2 + ci

    other = dev(z, y, 1 - core)
    yother = (y + 1) % Y

    def rc(src, s, sh, target, sem):
        return pltpu.make_async_remote_copy(
            src_ref=src, dst_ref=gath.at[s, :, sh], send_sem=sem, recv_sem=r_sem.at[s, sh],
            device_id={"tile": target}, device_id_type=MESH,
        )

    def arrived(s, sh):
        rc(gath.at[s, :, sh], s, sh, other, lc.at[s]).wait_recv()

    def small(src, dst, send, recv, target):
        return pltpu.make_async_remote_copy(
            src_ref=src, dst_ref=dst, send_sem=send, recv_sem=recv,
            device_id={"tile": target}, device_id_type=MESH,
        )

    def each(body, count):
        def step(i, carry):
            body(i)
            return carry
        lax.fori_loop(0, count, step, 0)

    def vis_copy(s, u):
        return pltpu.make_async_copy(vis.at[u, s], work.at[s, u], vsem.at[s, u])

    def res_copy(s, u):
        return pltpu.make_async_copy(work.at[s, u], res.at[u, s], osem.at[s, u])

    barrier = pltpu.get_barrier_semaphore()
    each(lambda k: pl.semaphore_signal(
        barrier, inc=1, device_id={"tile": (me + k + 1) % T}, device_id_type=MESH), T - 1)
    pl.semaphore_wait(barrier, T - 1)

    def up(src, s, zi):
        return rc(src, s, dev(zi, y, core), dev(z + 1, y, core), su.at[s, zi])

    def down(src, s, zi):
        return rc(src, s, dev(zi, y, core), dev(z - 1, y, core), sd.at[s, zi])

    def across(src, s, zi):
        return rc(src, s, dev(zi, y, core), dev(z, yother, core), sy.at[s, zi])

    def mate(src, s, zi, yi):
        return rc(src, s, dev(zi, yi, core), other, sc.at[s, zi * Y + yi])

    def own_step(s):
        src = own.at[s]

        @pl.when(z < Z - 1)
        def _():
            up(src, s, z).start()

        @pl.when(z > 0)
        def _():
            down(src, s, z).start()

        if Y > 1:
            across(src, s, z).start()
        mate(src, s, z, y).start()
        pltpu.make_async_copy(src, gath.at[s, :, me], lc.at[s]).start()

    each(own_step, slots)

    def bright_step(k):
        target = (me + k + 1) % T
        small(bright, ball.at[me], bs.at[k], br.at[me], target).start()
    each(bright_step, T - 1)
    ball[me] = bright[...]

    def vis_step(s):
        for u in range(units):
            vis_copy(s, u).start()
    each(vis_step, slots)
    flx[...] = jnp.zeros_like(flx)

    def z_step(d, s):
        @pl.when(z - d >= 0)
        def _():
            zi = z - d
            sh = dev(zi, y, core)
            arrived(s, sh)
            src = gath.at[s, :, sh]

            @pl.when(z < Z - 1)
            def _():
                up(src, s, zi).start()
            if Y > 1:
                across(src, s, zi).start()
            mate(src, s, zi, y).start()

        @pl.when(z + d < Z)
        def _():
            zi = z + d
            sh = dev(zi, y, core)
            arrived(s, sh)
            src = gath.at[s, :, sh]

            @pl.when(z > 0)
            def _():
                down(src, s, zi).start()
            if Y > 1:
                across(src, s, zi).start()
            mate(src, s, zi, y).start()

    def y_one(zi, s):
        sh = dev(zi, yother, core)
        arrived(s, sh)
        mate(gath.at[s, :, sh], s, zi, yother).start()

    def y_step(d, s):
        if Y == 1:
            return
        if d == 0:
            y_one(z, s)
            return
        pl.when(z - d >= 0)(lambda: y_one(z - d, s))
        pl.when(z + d < Z)(lambda: y_one(z + d, s))

    def hop_step(d, s):
        z_step(d, s)
        y_step(d - 1, s)

    for d in range(1, Z):
        each(functools.partial(hop_step, d), slots)

    def bright_wait(k):
        src = (me + k + 1) % T
        small(bright, ball.at[src], bs.at[k], br.at[src], other).wait_recv()
    each(bright_wait, T - 1)

    rows = T * 2 * per_group
    split = (T, 2, per_group, span)

    def turn(a):
        a4 = a.reshape(split)
        return jnp.concatenate([a4[:, 1:], -a4[:, :1]], axis=1).reshape(rows, span)

    def tn(a, b):
        return lax.dot_general(a, b, (((0,), (0,)), ((), ())), preferred_element_type=jnp.float32)

    def nt(a, b):
        return lax.dot_general(a, b, (((1,), (1,)), ((), ())), preferred_element_type=jnp.float32)

    def nn(a, b):
        return lax.dot_general(a, b, (((1,), (0,)), ((), ())), preferred_element_type=jnp.float32)

    def compute(s):
        lane = lax.broadcasted_iota(jnp.int32, (T, per_group, 128), 2)
        here = lane == s
        bcol = jnp.sum(jnp.where(here, ball[...].astype(jnp.float32), 0.0), axis=2, keepdims=True)

        def block(b):
            return gath[s, b].reshape(rows, span)

        def scaled_of(f):
            f4 = f.reshape(split).astype(jnp.float32)
            return (f4 * bcol[:, None]).astype(jnp.bfloat16).reshape(rows, span)

        def flag_rows(b):
            return jnp.broadcast_to(keep[s, b], (span, span)).T

        def add_flux(x, u, v):
            w = x.astype(jnp.float32) * u + turn(x).astype(jnp.float32) * v
            w = w.reshape(split)
            w = jnp.sum(w, axis=1)
            total = jnp.sum(w, axis=2, keepdims=True)
            flx[...] += jnp.where(here, total, 0.0)

        for u in range(units):
            p, q, diag = unit_blocks(me * units + u)
            vis_copy(s, u).wait()

            @pl.when(jnp.logical_not(diag))
            def _():
                x = block(p)
                c = block(q)
                sx = scaled_of(x)
                w = flag_rows(p) * keep[s, q]
                rre = (w * (work[s, u, 0].astype(jnp.float32) - tn(sx, c))).astype(jnp.bfloat16)
                rim = (w * (work[s, u, 1].astype(jnp.float32) - tn(turn(sx), c))).astype(jnp.bfloat16)
                work[s, u, 0] = rre
                work[s, u, 1] = rim
                add_flux(x, nt(c, rre), nt(c, rim))

            @pl.when(diag)
            def _():
                x = block(p)
                c = block(q)
                rid = lax.broadcasted_iota(jnp.int32, (span, span), 0)
                cid = lax.broadcasted_iota(jnp.int32, (span, span), 1)
                hi = rid < cid
                lo = rid > cid
                sx = scaled_of(x)
                sb = scaled_of(c)
                pre = jnp.where(hi, tn(sx, x), tn(c, sb))
                pim = jnp.where(hi, tn(turn(sx), x), tn(c, turn(sb)))
                w = jnp.where(hi, flag_rows(p) * keep[s, p], 0.0) + jnp.where(
                    lo, flag_rows(q) * keep[s, q], 0.0)
                rre = (w * (work[s, u, 0].astype(jnp.float32) - pre)).astype(jnp.bfloat16)
                rim = (w * (work[s, u, 1].astype(jnp.float32) - pim)).astype(jnp.bfloat16)
                work[s, u, 0] = rre
                work[s, u, 1] = rim
                zero = jnp.zeros((span, span), jnp.float32)
                def part(r, m):
                    return jnp.where(m, r.astype(jnp.float32), zero).astype(jnp.bfloat16)
                add_flux(x, nt(x, part(rre, hi)), nt(x, part(rim, hi)))
                add_flux(c, nn(c, part(rre, lo)), nn(c, part(rim, lo)))

            res_copy(s, u).start()


    def last_step(s):
        y_step(Z - 1, s)
        pltpu.make_async_copy(own.at[s], gath.at[s, :, me], lc.at[s]).wait()
        for i in range(T // 2):
            arrived(s, 2 * i + 1 - core)
        compute(s)

    each(last_step, slots)

    def flux_step(k):
        target = (me + k + 1) % T
        small(flx.at[target], frecv.at[me], fs.at[k], fr.at[me], target).start()
    each(flux_step, T - 1)
    frecv[me] = flx[me]

    def tidy(s):
        for u in range(units):
            res_copy(s, u).wait()
        for zi in range(Z):
            pl.when(jnp.logical_and(zi <= z, z < Z - 1))(lambda: up(own.at[s], s, zi).wait_send())
            pl.when(jnp.logical_and(zi >= z, z > 0))(lambda: down(own.at[s], s, zi).wait_send())
            if Y > 1:
                across(own.at[s], s, zi).wait_send()
            for yi in range(Y):
                mate(own.at[s], s, zi, yi).wait_send()
    each(tidy, slots)

    def small_wait(k):
        src = (me + k + 1) % T
        small(bright, ball.at[me], bs.at[k], br.at[me], src).wait_send()
        one = small(flx.at[src], frecv.at[src], fs.at[k], fr.at[src], src)
        one.wait_send()
        one.wait_recv()
    each(small_wait, T - 1)
    flux[...] = jnp.sum(frecv[...], axis=0) * scale


def per_device(
    layout, visibility, station_beam, antenna_uvw, source_dirs, source_flux, visible_list, antenna_flags
):
    Z, Y = layout
    T = lax.axis_size("tile")
    units, slots, _, span, _ = visibility.shape
    per_group = station_beam.shape[2]
    antennas = station_beam.shape[3]
    keep_all = 1.0 - antenna_flags.astype(jnp.float32)
    keep_all = keep_all.reshape(slots, BLOCKS, 1, span)
    own, brightness = build_factors(
        station_beam, antenna_uvw, source_dirs, source_flux, visible_list
    )
    bright = jnp.pad(brightness.T, ((0, 0), (0, 128 - slots)))
    dims = (Z, Y, slots, units, per_group, span, -1.0 / (8.0 * antennas))
    vmem = pl.BlockSpec(memory_space=pltpu.VMEM)
    hbm = pl.BlockSpec(memory_space=pl.ANY)
    dma = pltpu.SemaphoreType.DMA
    residual, flux = pl.pallas_call(
        functools.partial(kernel, dims),
        name="predict_pull",
        out_shape=(
            jax.ShapeDtypeStruct(visibility.shape, jnp.bfloat16),
            jax.ShapeDtypeStruct((per_group, 128), jnp.float32),
        ),
        in_specs=[vmem, vmem, vmem, hbm],
        out_specs=(hbm, vmem),
        scratch_shapes=[
            pltpu.VMEM((slots, BLOCKS, T, 2 * per_group, span), jnp.bfloat16),
            pltpu.VMEM((T, per_group, 128), jnp.bfloat16),
            pltpu.VMEM((slots, units, 2, span, span), jnp.bfloat16),
            pltpu.VMEM((T, per_group, 128), jnp.float32),
            pltpu.VMEM((T, per_group, 128), jnp.float32),
            dma((slots, T)),
            dma((slots, Z)),
            dma((slots, Z)),
            dma((slots, Z)),
            dma((slots, Z * Y)),
            dma((slots,)),
            dma((slots, units)),
            dma((slots, units)),
            dma((T,)),
            dma((T,)),
            dma((T,)),
            dma((T,)),
        ],
        compiler_params=pltpu.CompilerParams(
            collective_id=0, has_side_effects=True, vmem_limit_bytes=64 * 1024 * 1024 - 2 * 65536
        ),
    )(own, bright, keep_all, visibility)
    return residual, flux[:, :slots].T


def layout_of(mesh):
    count = mesh.shape["tile"]
    line = mesh.devices.reshape(-1, count)[0]
    places = [getattr(d, "coords", None) for d in line]
    fast = 1
    if all(c is not None for c in places):
        fast = max(1, len({tuple(c)[1] for c in places}))
    if (count // 2) % fast or fast > 2:
        fast = 1
    return count // 2 // fast, fast


def solution(mesh):
    return jax.shard_map(
        functools.partial(per_device, layout_of(mesh)),
        mesh=mesh,
        in_specs=(
            P("tile", "grp", None, None, None),
            P("grp", None, "tile", None),
            P("grp", None, None),
            P(None, "tile"),
            P(("grp", "tile")),
            P(None, "tile"),
            P("grp", None),
        ),
        out_specs=(P("tile", "grp", None, None, None), P("grp", "tile")),
        check_vma=False,
    )
```

```python
import functools
import math

import jax
import jax.numpy as jnp
from jax import lax
from jax.experimental import pallas as pl
from jax.experimental.pallas import tpu as pltpu
from jax.sharding import PartitionSpec as P

BLOCKS = 8
MESH = pl.DeviceIdType.MESH

two_pi = 2.0 * math.pi


def sin_cos_turns(turns):
    quarter = jnp.floor(turns * 4.0 + 0.5)
    angle = two_pi * (turns - quarter * 0.25)
    a2 = angle * angle
    sn = angle * (1.0 + a2 * (-1.0 / 6 + a2 * (1.0 / 120 + a2 * (-1.0 / 5040 + a2 * (1.0 / 362880)))))
    cs = 1.0 + a2 * (-0.5 + a2 * (1.0 / 24 + a2 * (-1.0 / 720 + a2 * (1.0 / 40320 - a2 * (1.0 / 3628800)))))
    kind = quarter - 4.0 * jnp.floor(quarter * 0.25)
    odd = jnp.logical_or(kind == 1.0, kind == 3.0)
    sine = jnp.where(odd, cs, sn)
    cosine = jnp.where(odd, sn, cs)
    sine = jnp.where(kind >= 2.0, -sine, sine)
    cosine = jnp.where(jnp.logical_or(kind == 1.0, kind == 2.0), -cosine, cosine)
    return sine, cosine


def unit_blocks(unit_id):
    pairs = BLOCKS * (BLOCKS - 1) // 2
    first = jnp.int32(0)
    start = jnp.int32(0)
    offset = 0
    for row in range(1, BLOCKS - 1):
        offset += BLOCKS - row
        first = jnp.where(unit_id >= offset, jnp.int32(row), first)
        start = jnp.where(unit_id >= offset, jnp.int32(offset), start)
    second = unit_id - start + first + 1
    diag = unit_id >= pairs
    first = jnp.where(diag, 2 * (unit_id - pairs), first)
    second = jnp.where(diag, 2 * (unit_id - pairs) + 1, second)
    return first, second, diag


def kernel(
    dims, beam, uvw, dirs, pool_flux, listed, flags, vis, res, flux,
    own, bacc, bright, gath, ball, work, flx, frecv,
    r_sem, su, sd, sy, sc, lc, vsem, osem, bs, br, fs, fr,
):
    Z, Y, slots, units, per_group, span, scale = dims
    T = Z * Y * 2
    me = lax.axis_index("tile")
    core = me % 2
    y = (me // 2) % Y
    z = me // (2 * Y)

    def dev(zi, yi, ci):
        return (zi * Y + yi) * 2 + ci

    other = dev(z, y, 1 - core)
    early = slots // 8 if Y > 1 else 0
    yother = (y + 1) % Y

    def rc(src, s, sh, target, sem):
        return pltpu.make_async_remote_copy(
            src_ref=src, dst_ref=gath.at[s, :, sh], send_sem=sem, recv_sem=r_sem.at[s, sh],
            device_id={"tile": target}, device_id_type=MESH,
        )

    def arrived(s, sh):
        rc(gath.at[s, :, sh], s, sh, other, lc.at[s]).wait_recv()

    def small(src, dst, send, recv, target):
        return pltpu.make_async_remote_copy(
            src_ref=src, dst_ref=dst, send_sem=send, recv_sem=recv,
            device_id={"tile": target}, device_id_type=MESH,
        )

    def each(body, count):
        def step(i, carry):
            body(i)
            return carry
        lax.fori_loop(0, count, step, 0)

    def vis_copy(s, u):
        return pltpu.make_async_copy(vis.at[u, s], work.at[s, u], vsem.at[s, u])

    def res_copy(s, u):
        return pltpu.make_async_copy(work.at[s, u], res.at[u, s], osem.at[s, u])

    barrier = pltpu.get_barrier_semaphore()
    each(lambda k: pl.semaphore_signal(
        barrier, inc=1, device_id={"tile": (me + k + 1) % T}, device_id_type=MESH), T - 1)

    def up(src, s, zi, yi):
        return rc(src, s, dev(zi, yi, core), dev(z + 1, y, core), su.at[s, zi * Y + yi])

    def down(src, s, zi, yi):
        return rc(src, s, dev(zi, yi, core), dev(z - 1, y, core), sd.at[s, zi * Y + yi])

    def onward(s, zi, yi, upward, downward):
        src = gath.at[s, :, dev(zi, yi, core)]
        if upward:
            pl.when(z < Z - 1)(lambda: up(src, s, zi, yi).start())
        if downward:
            pl.when(z > 0)(lambda: down(src, s, zi, yi).start())

    def across(src, s, zi):
        return rc(src, s, dev(zi, y, core), dev(z, yother, core), sy.at[s, zi])

    def mate(src, s, zi, yi):
        return rc(src, s, dev(zi, yi, core), other, sc.at[s, zi * Y + yi])

    def own_step(s):
        src = own.at[s]

        @pl.when(z < Z - 1)
        def _():
            up(src, s, z, y).start()

        @pl.when(z > 0)
        def _():
            down(src, s, z, y).start()

        if Y > 1:
            across(src, s, z).start()
        mate(src, s, z, y).start()
        pltpu.make_async_copy(src, gath.at[s, :, me], lc.at[s]).start()

    pool_size = dirs.shape[1]
    slot_lane = lax.broadcasted_iota(jnp.int32, (per_group, 128), 1)
    pool_lane = lax.broadcasted_iota(jnp.int32, (per_group, pool_size), 1).astype(jnp.float32)

    def make_factors(s):
        at_slot = slot_lane == s
        index = jnp.sum(jnp.where(at_slot, listed[...], 0.0), axis=1, keepdims=True)
        chosen = pool_lane == index

        def pick(row):
            return jnp.sum(jnp.where(chosen, row, 0.0), axis=1, keepdims=True)

        east = pick(dirs[0:1, :])
        north = pick(dirs[1:2, :])
        bacc[...] += jnp.where(at_slot, pick(pool_flux[...]), 0.0)
        depth = jnp.sqrt(1.0 - east * east - north * north) - 1.0
        for b in range(BLOCKS):
            cut = slice(b * span, (b + 1) * span)
            turns = uvw[s, 0:1, cut] * east + uvw[s, 1:2, cut] * north + uvw[s, 2:3, cut] * depth
            sine, cosine = sin_cos_turns(turns)
            b0 = beam[s, 0, :, cut].astype(jnp.float32)
            b1 = beam[s, 1, :, cut].astype(jnp.float32)
            own[s, b, :per_group] = (b0 * cosine + b1 * sine).astype(jnp.bfloat16)
            own[s, b, per_group:] = (b1 * cosine - b0 * sine).astype(jnp.bfloat16)

    bacc[...] = jnp.zeros_like(bacc)
    make_factors(0)
    pl.semaphore_wait(barrier, T - 1)

    def make_and_send(s):
        make_factors(s + 1)
        own_step(s)
    each(make_and_send, slots - 1)
    bright[...] = bacc[...].astype(jnp.bfloat16)
    flx[...] = jnp.zeros_like(flx)
    own_step(slots - 1)

    def bright_step(k):
        target = (me + k + 1) % T
        small(bright, ball.at[me], bs.at[k], br.at[me], target).start()
    each(bright_step, T - 1)
    ball[me] = bright[...]

    def vis_step(s):
        for u in range(units):
            vis_copy(s, u).start()
    each(vis_step, slots)

    def z_one(zi, s, upward):
        sh = dev(zi, y, core)
        arrived(s, sh)
        onward(s, zi, y, upward, not upward)
        if Y > 1:
            pl.when(s >= early)(lambda: across(gath.at[s, :, sh], s, zi).start())
        mate(gath.at[s, :, sh], s, zi, y).start()

    def z_step(d, s):
        pl.when(z - d >= 0)(lambda: z_one(z - d, s, True))
        pl.when(z + d < Z)(lambda: z_one(z + d, s, False))

    def y_one(zi, s, upward, downward):
        sh = dev(zi, yother, core)
        arrived(s, sh)
        if early:
            pl.when(s < early)(lambda: onward(s, zi, yother, upward, downward))
        mate(gath.at[s, :, sh], s, zi, yother).start()

    def y_step(d, s):
        if Y == 1:
            return
        if d == 0:
            y_one(z, s, True, True)
            return
        pl.when(z - d >= 0)(lambda: y_one(z - d, s, True, False))
        pl.when(z + d < Z)(lambda: y_one(z + d, s, False, True))

    def hop_step(d, s):
        z_step(d, s)
        y_step(d - 1, s)

    for d in range(1, Z):
        each(functools.partial(hop_step, d), slots)

    def bright_wait(k):
        src = (me + k + 1) % T
        small(bright, ball.at[src], bs.at[k], br.at[src], other).wait_recv()
    each(bright_wait, T - 1)

    rows = T * 2 * per_group
    split = (T, 2, per_group, span)

    def turn(a):
        a4 = a.reshape(split)
        return jnp.concatenate([a4[:, 1:], -a4[:, :1]], axis=1).reshape(rows, span)

    def tn(a, b):
        return lax.dot_general(a, b, (((0,), (0,)), ((), ())), preferred_element_type=jnp.float32)

    def nt(a, b):
        return lax.dot_general(a, b, (((1,), (1,)), ((), ())), preferred_element_type=jnp.float32)

    def nn(a, b):
        return lax.dot_general(a, b, (((1,), (0,)), ((), ())), preferred_element_type=jnp.float32)

    def compute(s):
        lane = lax.broadcasted_iota(jnp.int32, (T, per_group, 128), 2)
        here = lane == s
        bcol = jnp.sum(jnp.where(here, ball[...].astype(jnp.float32), 0.0), axis=2, keepdims=True)

        def block(b):
            return gath[s, b].reshape(rows, span)

        def scaled_of(f):
            f4 = f.reshape(split).astype(jnp.float32)
            return (f4 * bcol[:, None]).astype(jnp.bfloat16).reshape(rows, span)

        def keep_row(t, b):
            start = pl.multiple_of(b * span, span)
            return 1.0 - flags[pl.ds(t, 1), pl.ds(start, span)].astype(jnp.float32)

        def flag_rows(b):
            return jnp.broadcast_to(keep_row(s, b), (span, span)).T

        def add_flux(x, u, v):
            w = x.astype(jnp.float32) * u + turn(x).astype(jnp.float32) * v
            w = w.reshape(split)
            w = jnp.sum(w, axis=1)
            total = jnp.sum(w, axis=2, keepdims=True)
            flx[...] += jnp.where(here, total, 0.0)

        for u in range(units):
            p, q, diag = unit_blocks(me * units + u)
            vis_copy(s, u).wait()

            @pl.when(jnp.logical_not(diag))
            def _():
                x = block(p)
                c = block(q)
                sx = scaled_of(x)
                w = flag_rows(p) * keep_row(s, q)
                rre = (w * (work[s, u, 0].astype(jnp.float32) - tn(sx, c))).astype(jnp.bfloat16)
                rim = (w * (work[s, u, 1].astype(jnp.float32) - tn(turn(sx), c))).astype(jnp.bfloat16)
                work[s, u, 0] = rre
                work[s, u, 1] = rim
                add_flux(x, nt(c, rre), nt(c, rim))

            @pl.when(diag)
            def _():
                x = block(p)
                c = block(q)
                rid = lax.broadcasted_iota(jnp.int32, (span, span), 0)
                cid = lax.broadcasted_iota(jnp.int32, (span, span), 1)
                hi = rid < cid
                lo = rid > cid
                sx = scaled_of(x)
                sb = scaled_of(c)
                pre = jnp.where(hi, tn(sx, x), tn(c, sb))
                pim = jnp.where(hi, tn(turn(sx), x), tn(c, turn(sb)))
                w = jnp.where(hi, flag_rows(p) * keep_row(s, p), 0.0) + jnp.where(
                    lo, flag_rows(q) * keep_row(s, q), 0.0)
                rre = (w * (work[s, u, 0].astype(jnp.float32) - pre)).astype(jnp.bfloat16)
                rim = (w * (work[s, u, 1].astype(jnp.float32) - pim)).astype(jnp.bfloat16)
                work[s, u, 0] = rre
                work[s, u, 1] = rim
                zero = jnp.zeros((span, span), jnp.float32)
                def part(r, m):
                    return jnp.where(m, r.astype(jnp.float32), zero).astype(jnp.bfloat16)
                add_flux(x, nt(x, part(rre, hi)), nt(x, part(rim, hi)))
                add_flux(c, nn(c, part(rre, lo)), nn(c, part(rim, lo)))

            res_copy(s, u).start()


    def last_step(s):
        y_step(Z - 1, s)
        pltpu.make_async_copy(own.at[s], gath.at[s, :, me], lc.at[s]).wait()
        for i in range(T // 2):
            arrived(s, 2 * i + 1 - core)
        compute(s)

    each(last_step, slots)

    def flux_step(k):
        target = (me + k + 1) % T
        small(flx.at[target], frecv.at[me], fs.at[k], fr.at[me], target).start()
    each(flux_step, T - 1)
    frecv[me] = flx[me]

    def tidy(s):
        for u in range(units):
            res_copy(s, u).wait()
        def z_sent(zi, yi):
            src = own.at[s]
            pl.when(jnp.logical_and(zi <= z, z < Z - 1))(lambda: up(src, s, zi, yi).wait_send())
            pl.when(jnp.logical_and(zi >= z, z > 0))(lambda: down(src, s, zi, yi).wait_send())

        for zi in range(Z):
            z_sent(zi, y)
            if early:
                pl.when(s < early)(lambda: z_sent(zi, yother))
            if Y > 1:
                pl.when(jnp.logical_or(s >= early, zi == z))(
                    lambda: across(own.at[s], s, zi).wait_send())
            for yi in range(Y):
                mate(own.at[s], s, zi, yi).wait_send()
    each(tidy, slots)

    def small_wait(k):
        src = (me + k + 1) % T
        small(bright, ball.at[me], bs.at[k], br.at[me], src).wait_send()
        one = small(flx.at[src], frecv.at[src], fs.at[k], fr.at[src], src)
        one.wait_send()
        one.wait_recv()
    each(small_wait, T - 1)
    flux[...] = jnp.sum(frecv[...], axis=0) * scale


def per_device(
    layout, visibility, station_beam, antenna_uvw, source_dirs, source_flux, visible_list, antenna_flags
):
    Z, Y = layout
    T = lax.axis_size("tile")
    units, slots, _, span, _ = visibility.shape
    per_group = station_beam.shape[2]
    antennas = station_beam.shape[3]
    listed = jnp.pad(visible_list.astype(jnp.float32).T, ((0, 0), (0, 128 - slots)))
    pool_flux = source_flux.astype(jnp.float32)[None]
    dims = (Z, Y, slots, units, per_group, span, -1.0 / (8.0 * antennas))
    vmem = pl.BlockSpec(memory_space=pltpu.VMEM)
    hbm = pl.BlockSpec(memory_space=pl.ANY)
    dma = pltpu.SemaphoreType.DMA
    residual, flux = pl.pallas_call(
        functools.partial(kernel, dims),
        name="predict_pull",
        out_shape=(
            jax.ShapeDtypeStruct(visibility.shape, jnp.bfloat16),
            jax.ShapeDtypeStruct((per_group, 128), jnp.float32),
        ),
        in_specs=[vmem] * 6 + [hbm],
        out_specs=(hbm, vmem),
        scratch_shapes=[
            pltpu.VMEM((slots, BLOCKS, 2 * per_group, span), jnp.bfloat16),
            pltpu.VMEM((per_group, 128), jnp.float32),
            pltpu.VMEM((per_group, 128), jnp.bfloat16),
            pltpu.VMEM((slots, BLOCKS, T, 2 * per_group, span), jnp.bfloat16),
            pltpu.VMEM((T, per_group, 128), jnp.bfloat16),
            pltpu.VMEM((slots, units, 2, span, span), jnp.bfloat16),
            pltpu.VMEM((T, per_group, 128), jnp.float32),
            pltpu.VMEM((T, per_group, 128), jnp.float32),
            dma((slots, T)),
            dma((slots, Z * Y)),
            dma((slots, Z * Y)),
            dma((slots, Z)),
            dma((slots, Z * Y)),
            dma((slots,)),
            dma((slots, units)),
            dma((slots, units)),
            dma((T,)),
            dma((T,)),
            dma((T,)),
            dma((T,)),
        ],
        compiler_params=pltpu.CompilerParams(
            collective_id=0, has_side_effects=True, vmem_limit_bytes=64 * 1024 * 1024 - 2 * 65536
        ),
    )(station_beam, antenna_uvw, source_dirs, pool_flux, listed, antenna_flags, visibility)
    return residual, flux[:, :slots].T


def layout_of(mesh):
    count = mesh.shape["tile"]
    line = mesh.devices.reshape(-1, count)[0]
    places = [getattr(d, "coords", None) for d in line]
    fast = 1
    if all(c is not None for c in places):
        fast = max(1, len({tuple(c)[1] for c in places}))
    if (count // 2) % fast or fast > 2:
        fast = 1
    return count // 2 // fast, fast


def solution(mesh):
    return jax.shard_map(
        functools.partial(per_device, layout_of(mesh)),
        mesh=mesh,
        in_specs=(
            P("tile", "grp", None, None, None),
            P("grp", None, "tile", None),
            P("grp", None, None),
            P(None, "tile"),
            P(("grp", "tile")),
            P(None, "tile"),
            P("grp", None),
        ),
        out_specs=(P("tile", "grp", None, None, None), P("grp", "tile")),
        check_vma=False,
    )
```

```python
import functools
import math

import jax
import jax.numpy as jnp
from jax import lax
from jax.experimental import pallas as pl
from jax.experimental.pallas import tpu as pltpu
from jax.sharding import PartitionSpec as P

BLOCKS = 8
MESH = pl.DeviceIdType.MESH

two_pi = 2.0 * math.pi


def sin_cos_turns(turns):
    quarter = jnp.floor(turns * 4.0 + 0.5)
    angle = two_pi * (turns - quarter * 0.25)
    a2 = angle * angle
    sn = angle * (1.0 + a2 * (-1.0 / 6 + a2 * (1.0 / 120 + a2 * (-1.0 / 5040 + a2 * (1.0 / 362880)))))
    cs = 1.0 + a2 * (-0.5 + a2 * (1.0 / 24 + a2 * (-1.0 / 720 + a2 * (1.0 / 40320 - a2 * (1.0 / 3628800)))))
    kind = quarter - 4.0 * jnp.floor(quarter * 0.25)
    odd = jnp.logical_or(kind == 1.0, kind == 3.0)
    sine = jnp.where(odd, cs, sn)
    cosine = jnp.where(odd, sn, cs)
    sine = jnp.where(kind >= 2.0, -sine, sine)
    cosine = jnp.where(jnp.logical_or(kind == 1.0, kind == 2.0), -cosine, cosine)
    return sine, cosine


def unit_blocks(unit_id):
    pairs = BLOCKS * (BLOCKS - 1) // 2
    first = jnp.int32(0)
    start = jnp.int32(0)
    offset = 0
    for row in range(1, BLOCKS - 1):
        offset += BLOCKS - row
        first = jnp.where(unit_id >= offset, jnp.int32(row), first)
        start = jnp.where(unit_id >= offset, jnp.int32(offset), start)
    second = unit_id - start + first + 1
    diag = unit_id >= pairs
    first = jnp.where(diag, 2 * (unit_id - pairs), first)
    second = jnp.where(diag, 2 * (unit_id - pairs) + 1, second)
    return first, second, diag


def kernel(
    dims, beam, uvw, dirs, pool_flux, listed, flags, vis, res, flux,
    own, bacc, bright, gath, ball, work, flx, frecv,
    r_sem, su, sd, sy, sc, lc, vsem, osem, bs, br, fs, fr,
):
    Z, Y, slots, units, per_group, span, scale = dims
    T = Z * Y * 2
    me = lax.axis_index("tile")
    core = me % 2
    y = (me // 2) % Y
    z = me // (2 * Y)

    def dev(zi, yi, ci):
        return (zi * Y + yi) * 2 + ci

    other = dev(z, y, 1 - core)
    early = slots // 8 if Y > 1 else 0
    late_from = slots - early
    yother = (y + 1) % Y

    def rc(src, s, sh, target, sem):
        return pltpu.make_async_remote_copy(
            src_ref=src, dst_ref=gath.at[s, :, sh], send_sem=sem, recv_sem=r_sem.at[s, sh],
            device_id={"tile": target}, device_id_type=MESH,
        )

    def arrived(s, sh):
        rc(gath.at[s, :, sh], s, sh, other, lc.at[s]).wait_recv()

    def small(src, dst, send, recv, target):
        return pltpu.make_async_remote_copy(
            src_ref=src, dst_ref=dst, send_sem=send, recv_sem=recv,
            device_id={"tile": target}, device_id_type=MESH,
        )

    def each(body, count):
        def step(i, carry):
            body(i)
            return carry
        lax.fori_loop(0, count, step, 0)

    def vis_copy(s, u):
        return pltpu.make_async_copy(vis.at[u, s], work.at[s, u], vsem.at[s, u])

    def res_copy(s, u):
        return pltpu.make_async_copy(work.at[s, u], res.at[u, s], osem.at[s, u])

    barrier = pltpu.get_barrier_semaphore()
    each(lambda k: pl.semaphore_signal(
        barrier, inc=1, device_id={"tile": (me + k + 1) % T}, device_id_type=MESH), T - 1)

    def up(src, s, zi, yi):
        return rc(src, s, dev(zi, yi, core), dev(z + 1, y, core), su.at[s, zi * Y + yi])

    def down(src, s, zi, yi):
        return rc(src, s, dev(zi, yi, core), dev(z - 1, y, core), sd.at[s, zi * Y + yi])

    def onward(s, zi, yi, upward, downward):
        src = gath.at[s, :, dev(zi, yi, core)]
        if upward:
            pl.when(z < Z - 1)(lambda: up(src, s, zi, yi).start())
        if downward:
            pl.when(z > 0)(lambda: down(src, s, zi, yi).start())

    def across(src, s, zi):
        return rc(src, s, dev(zi, y, core), dev(z, yother, core), sy.at[s, zi])

    def mate(src, s, zi, yi):
        return rc(src, s, dev(zi, yi, core), other, sc.at[s, zi * Y + yi])

    def own_step(s):
        src = own.at[s]

        @pl.when(z < Z - 1)
        def _():
            up(src, s, z, y).start()

        @pl.when(z > 0)
        def _():
            down(src, s, z, y).start()

        if Y > 1:
            across(src, s, z).start()
        mate(src, s, z, y).start()
        pltpu.make_async_copy(src, gath.at[s, :, me], lc.at[s]).start()

    pool_size = dirs.shape[1]
    slot_lane = lax.broadcasted_iota(jnp.int32, (per_group, 128), 1)
    pool_lane = lax.broadcasted_iota(jnp.int32, (per_group, pool_size), 1).astype(jnp.float32)

    def make_factors(s):
        at_slot = slot_lane == s
        index = jnp.sum(jnp.where(at_slot, listed[...], 0.0), axis=1, keepdims=True)
        chosen = pool_lane == index

        def pick(row):
            return jnp.sum(jnp.where(chosen, row, 0.0), axis=1, keepdims=True)

        east = pick(dirs[0:1, :])
        north = pick(dirs[1:2, :])
        bacc[...] += jnp.where(at_slot, pick(pool_flux[...]), 0.0)
        depth = jnp.sqrt(1.0 - east * east - north * north) - 1.0
        for b in range(BLOCKS):
            cut = slice(b * span, (b + 1) * span)
            turns = uvw[s, 0:1, cut] * east + uvw[s, 1:2, cut] * north + uvw[s, 2:3, cut] * depth
            sine, cosine = sin_cos_turns(turns)
            b0 = beam[s, 0, :, cut].astype(jnp.float32)
            b1 = beam[s, 1, :, cut].astype(jnp.float32)
            own[s, b, :per_group] = (b0 * cosine + b1 * sine).astype(jnp.bfloat16)
            own[s, b, per_group:] = (b1 * cosine - b0 * sine).astype(jnp.bfloat16)

    bacc[...] = jnp.zeros_like(bacc)
    make_factors(0)
    pl.semaphore_wait(barrier, T - 1)

    def make_and_send(s):
        make_factors(s + 1)
        own_step(s)
    each(make_and_send, slots - 1)
    bright[...] = bacc[...].astype(jnp.bfloat16)
    flx[...] = jnp.zeros_like(flx)
    own_step(slots - 1)

    def bright_step(k):
        target = (me + k + 1) % T
        small(bright, ball.at[me], bs.at[k], br.at[me], target).start()
    each(bright_step, T - 1)
    ball[me] = bright[...]

    def vis_step(s):
        for u in range(units):
            vis_copy(s, u).start()
    each(vis_step, slots)

    def z_one(zi, s, upward):
        sh = dev(zi, y, core)
        arrived(s, sh)
        onward(s, zi, y, upward, not upward)
        if Y > 1:
            pl.when(s < late_from)(lambda: across(gath.at[s, :, sh], s, zi).start())
        mate(gath.at[s, :, sh], s, zi, y).start()

    def z_step(d, s):
        pl.when(z - d >= 0)(lambda: z_one(z - d, s, True))
        pl.when(z + d < Z)(lambda: z_one(z + d, s, False))

    def y_one(zi, s, upward, downward):
        sh = dev(zi, yother, core)
        arrived(s, sh)
        if early:
            pl.when(s >= late_from)(lambda: onward(s, zi, yother, upward, downward))
        mate(gath.at[s, :, sh], s, zi, yother).start()

    def y_step(d, s):
        if Y == 1:
            return
        if d == 0:
            y_one(z, s, True, True)
            return
        pl.when(z - d >= 0)(lambda: y_one(z - d, s, True, False))
        pl.when(z + d < Z)(lambda: y_one(z + d, s, False, True))

    def hop_step(d, s):
        z_step(d, s)
        y_step(d - 1, s)

    for d in range(1, Z):
        each(functools.partial(hop_step, d), slots)

    def bright_wait(k):
        src = (me + k + 1) % T
        small(bright, ball.at[src], bs.at[k], br.at[src], other).wait_recv()
    each(bright_wait, T - 1)

    rows = T * 2 * per_group
    split = (T, 2, per_group, span)

    def turn(a):
        a4 = a.reshape(split)
        return jnp.concatenate([a4[:, 1:], -a4[:, :1]], axis=1).reshape(rows, span)

    def tn(a, b):
        return lax.dot_general(a, b, (((0,), (0,)), ((), ())), preferred_element_type=jnp.float32)

    def nt(a, b):
        return lax.dot_general(a, b, (((1,), (1,)), ((), ())), preferred_element_type=jnp.float32)

    def nn(a, b):
        return lax.dot_general(a, b, (((1,), (0,)), ((), ())), preferred_element_type=jnp.float32)

    def compute(s):
        lane = lax.broadcasted_iota(jnp.int32, (T, per_group, 128), 2)
        here = lane == s
        bcol = jnp.sum(jnp.where(here, ball[...].astype(jnp.float32), 0.0), axis=2, keepdims=True)

        def block(b):
            return gath[s, b].reshape(rows, span)

        def scaled_of(f):
            f4 = f.reshape(split).astype(jnp.float32)
            return (f4 * bcol[:, None]).astype(jnp.bfloat16).reshape(rows, span)

        def keep_row(t, b):
            start = pl.multiple_of(b * span, span)
            return 1.0 - flags[pl.ds(t, 1), pl.ds(start, span)].astype(jnp.float32)

        def flag_rows(b):
            return jnp.broadcast_to(keep_row(s, b), (span, span)).T

        def add_flux(x, u, v):
            w = x.astype(jnp.float32) * u + turn(x).astype(jnp.float32) * v
            w = w.reshape(split)
            w = jnp.sum(w, axis=1)
            total = jnp.sum(w, axis=2, keepdims=True)
            flx[...] += jnp.where(here, total, 0.0)

        for u in range(units):
            p, q, diag = unit_blocks(me * units + u)
            vis_copy(s, u).wait()

            @pl.when(jnp.logical_not(diag))
            def _():
                x = block(p)
                c = block(q)
                sx = scaled_of(x)
                w = flag_rows(p) * keep_row(s, q)
                rre = (w * (work[s, u, 0].astype(jnp.float32) - tn(sx, c))).astype(jnp.bfloat16)
                rim = (w * (work[s, u, 1].astype(jnp.float32) - tn(turn(sx), c))).astype(jnp.bfloat16)
                work[s, u, 0] = rre
                work[s, u, 1] = rim
                add_flux(x, nt(c, rre), nt(c, rim))

            @pl.when(diag)
            def _():
                x = block(p)
                c = block(q)
                rid = lax.broadcasted_iota(jnp.int32, (span, span), 0)
                cid = lax.broadcasted_iota(jnp.int32, (span, span), 1)
                hi = rid < cid
                lo = rid > cid
                sx = scaled_of(x)
                sb = scaled_of(c)
                pre = jnp.where(hi, tn(sx, x), tn(c, sb))
                pim = jnp.where(hi, tn(turn(sx), x), tn(c, turn(sb)))
                w = jnp.where(hi, flag_rows(p) * keep_row(s, p), 0.0) + jnp.where(
                    lo, flag_rows(q) * keep_row(s, q), 0.0)
                rre = (w * (work[s, u, 0].astype(jnp.float32) - pre)).astype(jnp.bfloat16)
                rim = (w * (work[s, u, 1].astype(jnp.float32) - pim)).astype(jnp.bfloat16)
                work[s, u, 0] = rre
                work[s, u, 1] = rim
                zero = jnp.zeros((span, span), jnp.float32)
                def part(r, m):
                    return jnp.where(m, r.astype(jnp.float32), zero).astype(jnp.bfloat16)
                add_flux(x, nt(x, part(rre, hi)), nt(x, part(rim, hi)))
                add_flux(c, nn(c, part(rre, lo)), nn(c, part(rim, lo)))

            res_copy(s, u).start()


    def last_step(s):
        y_step(Z - 1, s)
        pltpu.make_async_copy(own.at[s], gath.at[s, :, me], lc.at[s]).wait()
        for i in range(T // 2):
            arrived(s, 2 * i + 1 - core)
        compute(s)

    each(last_step, slots)

    def flux_step(k):
        target = (me + k + 1) % T
        small(flx.at[target], frecv.at[me], fs.at[k], fr.at[me], target).start()
    each(flux_step, T - 1)
    frecv[me] = flx[me]

    def tidy(s):
        for u in range(units):
            res_copy(s, u).wait()
        def z_sent(zi, yi):
            src = own.at[s]
            pl.when(jnp.logical_and(zi <= z, z < Z - 1))(lambda: up(src, s, zi, yi).wait_send())
            pl.when(jnp.logical_and(zi >= z, z > 0))(lambda: down(src, s, zi, yi).wait_send())

        for zi in range(Z):
            z_sent(zi, y)
            if early:
                pl.when(s >= late_from)(lambda: z_sent(zi, yother))
            if Y > 1:
                pl.when(jnp.logical_or(s < late_from, zi == z))(
                    lambda: across(own.at[s], s, zi).wait_send())
            for yi in range(Y):
                mate(own.at[s], s, zi, yi).wait_send()
    each(tidy, slots)

    def small_wait(k):
        src = (me + k + 1) % T
        small(bright, ball.at[me], bs.at[k], br.at[me], src).wait_send()
        one = small(flx.at[src], frecv.at[src], fs.at[k], fr.at[src], src)
        one.wait_send()
        one.wait_recv()
    each(small_wait, T - 1)
    flux[...] = jnp.sum(frecv[...], axis=0) * scale


def per_device(
    layout, visibility, station_beam, antenna_uvw, source_dirs, source_flux, visible_list, antenna_flags
):
    Z, Y = layout
    T = lax.axis_size("tile")
    units, slots, _, span, _ = visibility.shape
    per_group = station_beam.shape[2]
    antennas = station_beam.shape[3]
    listed = jnp.pad(visible_list.astype(jnp.float32).T, ((0, 0), (0, 128 - slots)))
    pool_flux = source_flux.astype(jnp.float32)[None]
    dims = (Z, Y, slots, units, per_group, span, -1.0 / (8.0 * antennas))
    vmem = pl.BlockSpec(memory_space=pltpu.VMEM)
    hbm = pl.BlockSpec(memory_space=pl.ANY)
    dma = pltpu.SemaphoreType.DMA
    residual, flux = pl.pallas_call(
        functools.partial(kernel, dims),
        name="predict_pull",
        out_shape=(
            jax.ShapeDtypeStruct(visibility.shape, jnp.bfloat16),
            jax.ShapeDtypeStruct((per_group, 128), jnp.float32),
        ),
        in_specs=[vmem] * 6 + [hbm],
        out_specs=(hbm, vmem),
        scratch_shapes=[
            pltpu.VMEM((slots, BLOCKS, 2 * per_group, span), jnp.bfloat16),
            pltpu.VMEM((per_group, 128), jnp.float32),
            pltpu.VMEM((per_group, 128), jnp.bfloat16),
            pltpu.VMEM((slots, BLOCKS, T, 2 * per_group, span), jnp.bfloat16),
            pltpu.VMEM((T, per_group, 128), jnp.bfloat16),
            pltpu.VMEM((slots, units, 2, span, span), jnp.bfloat16),
            pltpu.VMEM((T, per_group, 128), jnp.float32),
            pltpu.VMEM((T, per_group, 128), jnp.float32),
            dma((slots, T)),
            dma((slots, Z * Y)),
            dma((slots, Z * Y)),
            dma((slots, Z)),
            dma((slots, Z * Y)),
            dma((slots,)),
            dma((slots, units)),
            dma((slots, units)),
            dma((T,)),
            dma((T,)),
            dma((T,)),
            dma((T,)),
        ],
        compiler_params=pltpu.CompilerParams(
            collective_id=0, has_side_effects=True, vmem_limit_bytes=64 * 1024 * 1024 - 2 * 65536
        ),
    )(station_beam, antenna_uvw, source_dirs, pool_flux, listed, antenna_flags, visibility)
    return residual, flux[:, :slots].T


def layout_of(mesh):
    count = mesh.shape["tile"]
    line = mesh.devices.reshape(-1, count)[0]
    places = [getattr(d, "coords", None) for d in line]
    fast = 1
    if all(c is not None for c in places):
        fast = max(1, len({tuple(c)[1] for c in places}))
    if (count // 2) % fast or fast > 2:
        fast = 1
    return count // 2 // fast, fast


def solution(mesh):
    return jax.shard_map(
        functools.partial(per_device, layout_of(mesh)),
        mesh=mesh,
        in_specs=(
            P("tile", "grp", None, None, None),
            P("grp", None, "tile", None),
            P("grp", None, None),
            P(None, "tile"),
            P(("grp", "tile")),
            P(None, "tile"),
            P("grp", None),
        ),
        out_specs=(P("tile", "grp", None, None, None), P("grp", "tile")),
        check_vma=False,
    )
```

```python
import functools
import math

import jax
import jax.numpy as jnp
from jax import lax
from jax.experimental import pallas as pl
from jax.experimental.pallas import tpu as pltpu
from jax.sharding import PartitionSpec as P

BLOCKS = 8
MESH = pl.DeviceIdType.MESH

two_pi = 2.0 * math.pi


def sin_cos_turns(turns):
    quarter = jnp.floor(turns * 4.0 + 0.5)
    angle = two_pi * (turns - quarter * 0.25)
    a2 = angle * angle
    sn = angle * (1.0 + a2 * (-1.0 / 6 + a2 * (1.0 / 120 + a2 * (-1.0 / 5040 + a2 * (1.0 / 362880)))))
    cs = 1.0 + a2 * (-0.5 + a2 * (1.0 / 24 + a2 * (-1.0 / 720 + a2 * (1.0 / 40320 - a2 * (1.0 / 3628800)))))
    kind = quarter - 4.0 * jnp.floor(quarter * 0.25)
    odd = jnp.logical_or(kind == 1.0, kind == 3.0)
    sine = jnp.where(odd, cs, sn)
    cosine = jnp.where(odd, sn, cs)
    sine = jnp.where(kind >= 2.0, -sine, sine)
    cosine = jnp.where(jnp.logical_or(kind == 1.0, kind == 2.0), -cosine, cosine)
    return sine, cosine


def unit_blocks(unit_id):
    pairs = BLOCKS * (BLOCKS - 1) // 2
    first = jnp.int32(0)
    start = jnp.int32(0)
    offset = 0
    for row in range(1, BLOCKS - 1):
        offset += BLOCKS - row
        first = jnp.where(unit_id >= offset, jnp.int32(row), first)
        start = jnp.where(unit_id >= offset, jnp.int32(offset), start)
    second = unit_id - start + first + 1
    diag = unit_id >= pairs
    first = jnp.where(diag, 2 * (unit_id - pairs), first)
    second = jnp.where(diag, 2 * (unit_id - pairs) + 1, second)
    return first, second, diag


def kernel(
    dims, beam, uvw, dirs, pool_flux, listed, flags, vis, res, flux,
    own, bacc, bright, gath, ball, work, flx, frecv,
    r_sem, su, sd, sy, sc, lc, vsem, osem, bs, br, fs, fr,
):
    Z, Y, slots, units, per_group, span, scale = dims
    T = Z * Y * 2
    me = lax.axis_index("tile")
    core = me % 2
    y = (me // 2) % Y
    z = me // (2 * Y)

    def dev(zi, yi, ci):
        return (zi * Y + yi) * 2 + ci

    other = dev(z, y, 1 - core)
    early = slots // 8 if Y > 1 else 0
    late_from = slots - early
    yother = (y + 1) % Y

    def rc(src, s, sh, target, sem):
        return pltpu.make_async_remote_copy(
            src_ref=src, dst_ref=gath.at[s, :, sh], send_sem=sem, recv_sem=r_sem.at[s, sh],
            device_id={"tile": target}, device_id_type=MESH,
        )

    def arrived(s, sh):
        rc(gath.at[s, :, sh], s, sh, other, lc.at[s]).wait_recv()

    def small(src, dst, send, recv, target):
        return pltpu.make_async_remote_copy(
            src_ref=src, dst_ref=dst, send_sem=send, recv_sem=recv,
            device_id={"tile": target}, device_id_type=MESH,
        )

    def each(body, count):
        def step(i, carry):
            body(i)
            return carry
        lax.fori_loop(0, count, step, 0)

    def vis_copy(s, u):
        return pltpu.make_async_copy(vis.at[u, s], work.at[s, u], vsem.at[s, u])

    def res_copy(s, u):
        return pltpu.make_async_copy(work.at[s, u], res.at[u, s], osem.at[s, u])

    barrier = pltpu.get_barrier_semaphore()
    each(lambda k: pl.semaphore_signal(
        barrier, inc=1, device_id={"tile": (me + k + 1) % T}, device_id_type=MESH), T - 1)

    def up(src, s, zi, yi):
        return rc(src, s, dev(zi, yi, core), dev(z + 1, y, core), su.at[s, zi * Y + yi])

    def down(src, s, zi, yi):
        return rc(src, s, dev(zi, yi, core), dev(z - 1, y, core), sd.at[s, zi * Y + yi])

    def onward(s, zi, yi, upward, downward):
        src = gath.at[s, :, dev(zi, yi, core)]
        if upward:
            pl.when(z < Z - 1)(lambda: up(src, s, zi, yi).start())
        if downward:
            pl.when(z > 0)(lambda: down(src, s, zi, yi).start())

    def across(src, s, zi):
        return rc(src, s, dev(zi, y, core), dev(z, yother, core), sy.at[s, zi])

    def mate(src, s, zi, yi):
        return rc(src, s, dev(zi, yi, core), other, sc.at[s, zi * Y + yi])

    def own_step(s):
        src = own.at[s]

        @pl.when(z < Z - 1)
        def _():
            up(src, s, z, y).start()

        @pl.when(z > 0)
        def _():
            down(src, s, z, y).start()

        if Y > 1:
            across(src, s, z).start()
        mate(src, s, z, y).start()
        pltpu.make_async_copy(src, gath.at[s, :, me], lc.at[s]).start()

    pool_size = dirs.shape[1]
    slot_lane = lax.broadcasted_iota(jnp.int32, (per_group, 128), 1)
    pool_lane = lax.broadcasted_iota(jnp.int32, (per_group, pool_size), 1).astype(jnp.float32)

    def make_factors(s):
        at_slot = slot_lane == s
        index = jnp.sum(jnp.where(at_slot, listed[...], 0.0), axis=1, keepdims=True)
        chosen = pool_lane == index

        def pick(row):
            return jnp.sum(jnp.where(chosen, row, 0.0), axis=1, keepdims=True)

        east = pick(dirs[0:1, :])
        north = pick(dirs[1:2, :])
        bacc[...] += jnp.where(at_slot, pick(pool_flux[...]), 0.0)
        depth = jnp.sqrt(1.0 - east * east - north * north) - 1.0
        for b in range(BLOCKS):
            cut = slice(b * span, (b + 1) * span)
            turns = uvw[s, 0:1, cut] * east + uvw[s, 1:2, cut] * north + uvw[s, 2:3, cut] * depth
            sine, cosine = sin_cos_turns(turns)
            b0 = beam[s, 0, :, cut].astype(jnp.float32)
            b1 = beam[s, 1, :, cut].astype(jnp.float32)
            own[s, b, :per_group] = (b0 * cosine + b1 * sine).astype(jnp.bfloat16)
            own[s, b, per_group:] = (b1 * cosine - b0 * sine).astype(jnp.bfloat16)

    bacc[...] = jnp.zeros_like(bacc)
    make_factors(0)
    pl.semaphore_wait(barrier, T - 1)

    def make_and_send(s):
        make_factors(s + 1)
        own_step(s)
    each(make_and_send, slots - 1)
    bright[...] = bacc[...].astype(jnp.bfloat16)
    flx[...] = jnp.zeros_like(flx)
    own_step(slots - 1)

    def bright_step(k):
        target = (me + k + 1) % T
        small(bright, ball.at[me], bs.at[k], br.at[me], target).start()
    each(bright_step, T - 1)
    ball[me] = bright[...]

    def vis_step(s):
        for u in range(units):
            vis_copy(s, u).start()
    each(vis_step, slots)

    def z_one(zi, s, upward):
        sh = dev(zi, y, core)
        arrived(s, sh)
        onward(s, zi, y, upward, not upward)
        if Y > 1:
            pl.when(s < late_from)(lambda: across(gath.at[s, :, sh], s, zi).start())
        mate(gath.at[s, :, sh], s, zi, y).start()

    def z_step(d, s):
        pl.when(z - d >= 0)(lambda: z_one(z - d, s, True))
        pl.when(z + d < Z)(lambda: z_one(z + d, s, False))

    def y_one(zi, s, upward, downward):
        sh = dev(zi, yother, core)
        arrived(s, sh)
        if early:
            pl.when(s >= late_from)(lambda: onward(s, zi, yother, upward, downward))
        mate(gath.at[s, :, sh], s, zi, yother).start()

    def y_step(d, s):
        if Y == 1:
            return
        if d == 0:
            y_one(z, s, True, True)
            return
        pl.when(z - d >= 0)(lambda: y_one(z - d, s, True, False))
        pl.when(z + d < Z)(lambda: y_one(z + d, s, False, True))

    def hop_step(d, s):
        z_step(d, s)
        y_step(d - 1, s)

    for d in range(1, Z - 1):
        each(functools.partial(hop_step, d), slots)

    def bright_wait(k):
        src = (me + k + 1) % T
        small(bright, ball.at[src], bs.at[k], br.at[src], other).wait_recv()
    each(bright_wait, T - 1)

    rows = T * 2 * per_group
    split = (T, 2, per_group, span)

    def turn(a):
        a4 = a.reshape(split)
        return jnp.concatenate([a4[:, 1:], -a4[:, :1]], axis=1).reshape(rows, span)

    def tn(a, b):
        return lax.dot_general(a, b, (((0,), (0,)), ((), ())), preferred_element_type=jnp.float32)

    def nt(a, b):
        return lax.dot_general(a, b, (((1,), (1,)), ((), ())), preferred_element_type=jnp.float32)

    def nn(a, b):
        return lax.dot_general(a, b, (((1,), (0,)), ((), ())), preferred_element_type=jnp.float32)

    def compute(s):
        lane = lax.broadcasted_iota(jnp.int32, (T, per_group, 128), 2)
        here = lane == s
        bcol = jnp.sum(jnp.where(here, ball[...].astype(jnp.float32), 0.0), axis=2, keepdims=True)

        def block(b):
            return gath[s, b].reshape(rows, span)

        def scaled_of(f):
            f4 = f.reshape(split).astype(jnp.float32)
            return (f4 * bcol[:, None]).astype(jnp.bfloat16).reshape(rows, span)

        def keep_row(t, b):
            start = pl.multiple_of(b * span, span)
            return 1.0 - flags[pl.ds(t, 1), pl.ds(start, span)].astype(jnp.float32)

        def flag_rows(b):
            return jnp.broadcast_to(keep_row(s, b), (span, span)).T

        def add_flux(x, u, v):
            w = x.astype(jnp.float32) * u + turn(x).astype(jnp.float32) * v
            w = w.reshape(split)
            w = jnp.sum(w, axis=1)
            total = jnp.sum(w, axis=2, keepdims=True)
            flx[...] += jnp.where(here, total, 0.0)

        for u in range(units):
            p, q, diag = unit_blocks(me * units + u)
            vis_copy(s, u).wait()

            @pl.when(jnp.logical_not(diag))
            def _():
                x = block(p)
                c = block(q)
                sx = scaled_of(x)
                w = flag_rows(p) * keep_row(s, q)
                rre = (w * (work[s, u, 0].astype(jnp.float32) - tn(sx, c))).astype(jnp.bfloat16)
                rim = (w * (work[s, u, 1].astype(jnp.float32) - tn(turn(sx), c))).astype(jnp.bfloat16)
                work[s, u, 0] = rre
                work[s, u, 1] = rim
                add_flux(x, nt(c, rre), nt(c, rim))

            @pl.when(diag)
            def _():
                x = block(p)
                c = block(q)
                rid = lax.broadcasted_iota(jnp.int32, (span, span), 0)
                cid = lax.broadcasted_iota(jnp.int32, (span, span), 1)
                hi = rid < cid
                lo = rid > cid
                sx = scaled_of(x)
                sb = scaled_of(c)
                pre = jnp.where(hi, tn(sx, x), tn(c, sb))
                pim = jnp.where(hi, tn(turn(sx), x), tn(c, turn(sb)))
                w = jnp.where(hi, flag_rows(p) * keep_row(s, p), 0.0) + jnp.where(
                    lo, flag_rows(q) * keep_row(s, q), 0.0)
                rre = (w * (work[s, u, 0].astype(jnp.float32) - pre)).astype(jnp.bfloat16)
                rim = (w * (work[s, u, 1].astype(jnp.float32) - pim)).astype(jnp.bfloat16)
                work[s, u, 0] = rre
                work[s, u, 1] = rim
                zero = jnp.zeros((span, span), jnp.float32)
                def part(r, m):
                    return jnp.where(m, r.astype(jnp.float32), zero).astype(jnp.bfloat16)
                add_flux(x, nt(x, part(rre, hi)), nt(x, part(rim, hi)))
                add_flux(c, nn(c, part(rre, lo)), nn(c, part(rim, lo)))

            res_copy(s, u).start()


    def last_step(s):
        y_step(Z - 1, s)
        pltpu.make_async_copy(own.at[s], gath.at[s, :, me], lc.at[s]).wait()
        for i in range(T // 2):
            arrived(s, 2 * i + 1 - core)
        compute(s)

    def far_step(s):
        if Z > 1:
            pl.when(s < slots)(lambda: hop_step(Z - 1, s))
        pl.when(s > 0)(lambda: last_step(s - 1))

    each(far_step, slots + 1)

    def flux_step(k):
        target = (me + k + 1) % T
        small(flx.at[target], frecv.at[me], fs.at[k], fr.at[me], target).start()
    each(flux_step, T - 1)
    frecv[me] = flx[me]

    def tidy(s):
        for u in range(units):
            res_copy(s, u).wait()
        def z_sent(zi, yi):
            src = own.at[s]
            pl.when(jnp.logical_and(zi <= z, z < Z - 1))(lambda: up(src, s, zi, yi).wait_send())
            pl.when(jnp.logical_and(zi >= z, z > 0))(lambda: down(src, s, zi, yi).wait_send())

        for zi in range(Z):
            z_sent(zi, y)
            if early:
                pl.when(s >= late_from)(lambda: z_sent(zi, yother))
            if Y > 1:
                pl.when(jnp.logical_or(s < late_from, zi == z))(
                    lambda: across(own.at[s], s, zi).wait_send())
            for yi in range(Y):
                mate(own.at[s], s, zi, yi).wait_send()
    each(tidy, slots)

    def small_wait(k):
        src = (me + k + 1) % T
        small(bright, ball.at[me], bs.at[k], br.at[me], src).wait_send()
        one = small(flx.at[src], frecv.at[src], fs.at[k], fr.at[src], src)
        one.wait_send()
        one.wait_recv()
    each(small_wait, T - 1)
    flux[...] = jnp.sum(frecv[...], axis=0) * scale


def per_device(
    layout, visibility, station_beam, antenna_uvw, source_dirs, source_flux, visible_list, antenna_flags
):
    Z, Y = layout
    T = lax.axis_size("tile")
    units, slots, _, span, _ = visibility.shape
    per_group = station_beam.shape[2]
    antennas = station_beam.shape[3]
    listed = jnp.pad(visible_list.astype(jnp.float32).T, ((0, 0), (0, 128 - slots)))
    pool_flux = source_flux.astype(jnp.float32)[None]
    dims = (Z, Y, slots, units, per_group, span, -1.0 / (8.0 * antennas))
    vmem = pl.BlockSpec(memory_space=pltpu.VMEM)
    hbm = pl.BlockSpec(memory_space=pl.ANY)
    dma = pltpu.SemaphoreType.DMA
    residual, flux = pl.pallas_call(
        functools.partial(kernel, dims),
        name="predict_pull",
        out_shape=(
            jax.ShapeDtypeStruct(visibility.shape, jnp.bfloat16),
            jax.ShapeDtypeStruct((per_group, 128), jnp.float32),
        ),
        in_specs=[vmem] * 6 + [hbm],
        out_specs=(hbm, vmem),
        scratch_shapes=[
            pltpu.VMEM((slots, BLOCKS, 2 * per_group, span), jnp.bfloat16),
            pltpu.VMEM((per_group, 128), jnp.float32),
            pltpu.VMEM((per_group, 128), jnp.bfloat16),
            pltpu.VMEM((slots, BLOCKS, T, 2 * per_group, span), jnp.bfloat16),
            pltpu.VMEM((T, per_group, 128), jnp.bfloat16),
            pltpu.VMEM((slots, units, 2, span, span), jnp.bfloat16),
            pltpu.VMEM((T, per_group, 128), jnp.float32),
            pltpu.VMEM((T, per_group, 128), jnp.float32),
            dma((slots, T)),
            dma((slots, Z * Y)),
            dma((slots, Z * Y)),
            dma((slots, Z)),
            dma((slots, Z * Y)),
            dma((slots,)),
            dma((slots, units)),
            dma((slots, units)),
            dma((T,)),
            dma((T,)),
            dma((T,)),
            dma((T,)),
        ],
        compiler_params=pltpu.CompilerParams(
            collective_id=0, has_side_effects=True, vmem_limit_bytes=64 * 1024 * 1024 - 2 * 65536
        ),
    )(station_beam, antenna_uvw, source_dirs, pool_flux, listed, antenna_flags, visibility)
    return residual, flux[:, :slots].T


def layout_of(mesh):
    count = mesh.shape["tile"]
    line = mesh.devices.reshape(-1, count)[0]
    places = [getattr(d, "coords", None) for d in line]
    fast = 1
    if all(c is not None for c in places):
        fast = max(1, len({tuple(c)[1] for c in places}))
    if (count // 2) % fast or fast > 2:
        fast = 1
    return count // 2 // fast, fast


def solution(mesh):
    return jax.shard_map(
        functools.partial(per_device, layout_of(mesh)),
        mesh=mesh,
        in_specs=(
            P("tile", "grp", None, None, None),
            P("grp", None, "tile", None),
            P("grp", None, None),
            P(None, "tile"),
            P(("grp", "tile")),
            P(None, "tile"),
            P("grp", None),
        ),
        out_specs=(P("tile", "grp", None, None, None), P("grp", "tile")),
        check_vma=False,
    )
```
